512 devices in a mesh: center: 128 (over x, z, core), batch: 4 (over y).
Axes of the slice: x: 4, y: 4, z: 16, core: 2. Of those that a mesh axis runs over, the one named last changes fastest.
Arguments:
- centers: bfloat16 [65536, 384], P('center'), may hold values from -4 to 4
- weights: bfloat16 [65536, 512], P('center'), may hold values from -1 to 1
- subset_index: int32 [12288], P('center'), may hold values from 0 to 65535, as said below
- basis: bfloat16 [12288, 256], P('center'), may hold values from -2 to 2
- damping: float32 [256], replicated, may hold values from 0.2 to 0.95
- stored_train_features: bfloat16 [4, 8192, 384], P('batch', 'center'), may hold values from -4 to 4
- pool_labels: bfloat16 [4, 8192, 512], P('batch', 'center'), may hold values from -4 to 4
- picks: int32 [4, 256], P('batch', 'center'), may hold values from 0 to 63
Outputs:
- new_weights: bfloat16 [65536, 512], P('center')
- residual: bfloat16 [4, 256, 512], P('batch', 'center')
The draws below stay inside these ranges and needn't reach their ends.
Inputs may be any that keep to these rules, and one draw needn't show every extreme that they name: `subset_index`: the entries are distinct centers; center p is held by index p // 512 of center. Of the 96 entries on one device at most 3 are held by any one index, and in every draw some index holds exactly 3 of the entries of every device.
All inputs are finite; a program needn't handle non-finite values.
Results may differ from the reference program's by a relative error of at most 0.013.
Values may be sent and summed in bfloat16 or wider, within the bound.
No kernel may reach another device: no remote copies, remote signals or barrier semaphores. Data moves between devices by JAX's collectives and lax.ppermute only.
A program may use at most 64 MiB of HBM per device.

```python
import math
import jax
import jax.numpy as jnp
from jax import lax

D = 384
C = 512
Q = 256
PC = 512
BS_DEV = 2
POOL_DEV = 64
S_DEV = 96
P_SIZE = 65536
S = 12288
CAP = 3
GROUPS = 4
BG = 256
POOL_GROUP = 8192
N_CENTER = 128


cluster_count = 256


def cluster_table(key):
    table_key = jax.random.fold_in(key, 13)
    values = jnp.clip(jax.random.normal(table_key, (cluster_count, D), jnp.float32), -4.0, 4.0)
    return values * (18.0 / D) ** 0.5


def feature_values(key, own_constant, leading_shape):
    mean_table = cluster_table(key)
    id_key, noise_key = jax.random.split(jax.random.fold_in(key, own_constant), 2)
    cluster_ids = jax.random.randint(id_key, leading_shape, 0, cluster_count, dtype=jnp.int32)
    full_shape = leading_shape + (D,)
    noise_values = jnp.clip(jax.random.normal(noise_key, full_shape, jnp.float32), -4.0, 4.0)
    values = mean_table[cluster_ids] + noise_values * (0.32 / D) ** 0.5
    return jnp.clip(values, -4.0, 4.0).astype(jnp.bfloat16)


def draw_centers(key, part):
    return feature_values(key, 3, (P_SIZE,))


def draw_stored_train_features(key, part):
    return feature_values(key, 5, (GROUPS, POOL_GROUP))


def draw_weights(key, part):
    first_key = jax.random.fold_in(jax.random.fold_in(key, 17), 0)
    magnitude = float(P_SIZE // 16) ** (-0.5)
    values = jnp.clip(jax.random.normal(first_key, (P_SIZE, C), jnp.float32), -4.0, 4.0)
    values = values * magnitude
    return (values - jnp.roll(values, 1, axis=0)).astype(jnp.bfloat16)


def draw_basis(key, part):
    holders = S // S_DEV
    first_key, second_key = jax.random.split(jax.random.fold_in(key, 7))
    magnitude = 1.2 * float(S * Q) ** (-0.25)
    values = jnp.clip(jax.random.normal(first_key, (S, Q), jnp.float32), -4.0, 4.0)
    pairing = jax.random.permutation(second_key, holders)
    row_holder = jnp.arange(S, dtype=jnp.int32) // S_DEV
    column_block = jnp.arange(Q, dtype=jnp.int32) // (Q // holders)
    spike = jnp.where(pairing[row_holder][:, None] == column_block[None, :], 4.0, 1.0)
    return (values * magnitude * spike).astype(jnp.bfloat16)


def draw_subset_index(key, part):
    holders = S // S_DEV
    slot_count = holders * CAP
    keys = jax.random.split(jax.random.fold_in(key, 11), 4)
    busiest = jax.random.randint(keys[0], (), 0, holders, dtype=jnp.int32)
    owner_bias = jax.random.randint(keys[1], (holders,), 0, 2048, dtype=jnp.int32)
    shuffles = jax.vmap(lambda subkey: jax.random.permutation(subkey, PC))(jax.random.split(keys[2], holders))
    slot_ids = jnp.arange(slot_count, dtype=jnp.int32)
    slot_holder = slot_ids // CAP

    def single_provider(subkey, source):
        jitter_key, order_key = jax.random.split(subkey)
        jitter = jax.random.randint(jitter_key, (slot_count,), 0, 4096, dtype=jnp.int32)
        ranking = owner_bias[slot_holder] + jitter
        ranking = jnp.where(slot_holder == busiest, 16384, ranking)
        ranking = ranking * slot_count + slot_ids
        _, chosen = lax.top_k(ranking, S_DEV)
        chosen = chosen.astype(jnp.int32)
        holder = chosen // CAP
        inside_slice = chosen - holder * CAP
        local_row = shuffles[holder, source * CAP + inside_slice].astype(jnp.int32)
        entries = holder * PC + local_row
        position_order = jax.random.permutation(order_key, S_DEV)
        return entries[position_order]
    sources = jnp.arange(holders, dtype=jnp.int32)
    result = jax.vmap(single_provider)(jax.random.split(keys[3], holders), sources)
    return result.reshape(S).astype(jnp.int32)


def with_ends(values, key, least, largest):
    index_at = [jax.random.randint(jax.random.fold_in(key, axis), (), 0, length) for axis, length in enumerate(values.shape)]
    main_axis = values.shape.index(max(values.shape))
    next_to = index_at[:main_axis] + [(index_at[main_axis] + 1) % values.shape[main_axis]] + index_at[main_axis + 1:]
    return values.at[tuple(index_at)].set(least).at[tuple(next_to)].set(largest)


def steps_of(own_key, shape, pieces, least, largest):
    def one(axis_at, shards_of):
        steps = jax.random.uniform(jax.random.fold_in(jax.random.fold_in(own_key, 6), axis_at), (shards_of,), jnp.float32, least / len(pieces), largest / len(pieces))
        return jnp.repeat(jnp.exp(steps), shape[axis_at] // shards_of).reshape((-1,) + (1,) * (len(shape) - axis_at - 1))

    level = one(*pieces[0])
    for cut in pieces[1:]:
        level = level * one(*cut)
    return level


def bell_draw(rng, dims, deviation, limit, cuts=(), kind=jnp.bfloat16):
    values = deviation * jax.random.normal(rng, dims, jnp.float32)
    if cuts:
        values = values * steps_of(rng, dims, cuts, -0.22, 0.18)
    return jnp.clip(values, -limit, limit).astype(kind)


def setup_inputs(seed: int = 0) -> dict:
    streams_of = jax.random.split(jax.random.key(seed), 9)
    centers = draw_centers(jax.random.fold_in(streams_of[8], 71), 0)
    weights = draw_weights(jax.random.fold_in(streams_of[8], 71), 0)
    subset_index = draw_subset_index(jax.random.fold_in(streams_of[8], 71), 0)
    basis = draw_basis(jax.random.fold_in(streams_of[8], 71), 0)
    damping = jnp.clip(jnp.exp(jax.random.uniform(streams_of[4], (Q,), jnp.float32, math.log(0.2), math.log(0.95))), 0.2, 0.95)
    stored_train_features = draw_stored_train_features(jax.random.fold_in(streams_of[8], 71), 0)
    pool_labels = bell_draw(streams_of[6], (GROUPS, POOL_GROUP, C), 1.0, 4.0, ((0, 4), (1, 128)))
    picks = with_ends(jax.random.randint(streams_of[7], (GROUPS, BG), 0, POOL_DEV), jax.random.fold_in(streams_of[7], 1), 0, POOL_DEV - 1).astype(jnp.int32)
    return dict(centers=centers, weights=weights, subset_index=subset_index, basis=basis, damping=damping, stored_train_features=stored_train_features, pool_labels=pool_labels, picks=picks)


kernel_length = 2.0
step_rate = 0.1

def kernel_block(features, sample_squared_norm, center_rows):
    centers_sq = lax.optimization_barrier(jnp.sum(jnp.square(center_rows.astype(jnp.float32)), axis=1))
    cross = jnp.dot(features, center_rows.T, preferred_element_type=jnp.float32)
    distance = sample_squared_norm[:, None] + centers_sq[None, :] - 2.0 * cross
    return jnp.exp(-jnp.sqrt(jnp.maximum(distance, 0.0)) / kernel_length).astype(jnp.bfloat16)

def reference(centers, weights, subset_index, basis, damping, stored_train_features, pool_labels, picks):
    groups = stored_train_features.shape[0]
    position = jnp.arange(BG, dtype=jnp.int32) // BS_DEV * POOL_DEV
    position = position[None, :] + picks.astype(jnp.int32)
    features = jax.vmap(lambda pool_rows, indices: jnp.take(pool_rows, indices, axis=0))(stored_train_features, position)
    targets = jax.vmap(lambda pool_rows, indices: jnp.take(pool_rows, indices, axis=0))(pool_labels, position)
    flat_features = features.reshape(groups * BG, D)
    sample_squared_norm = lax.optimization_barrier(jnp.sum(jnp.square(flat_features.astype(jnp.float32)), axis=1))
    center_blocks = centers.reshape(N_CENTER, PC, D)
    weight_blocks = weights.reshape(N_CENTER, PC, C)

    def predict(running, operands):
        center_rows, weight_rows = operands
        laplace_kernel = kernel_block(flat_features, sample_squared_norm, center_rows)
        return (running + jnp.dot(laplace_kernel, weight_rows, preferred_element_type=jnp.float32), None)
    predicted, _ = lax.scan(predict, jnp.zeros((groups * BG, C), jnp.float32), (center_blocks, weight_blocks))
    residual = (predicted - targets.reshape(groups * BG, C).astype(jnp.float32)).astype(jnp.bfloat16)
    residual = residual.reshape(groups, BG, C)

    def gradient(running, center_rows):
        laplace_kernel = kernel_block(flat_features, sample_squared_norm, center_rows).reshape(groups, BG, PC)
        subtotal_sums = jnp.einsum('jwy,jwu->jyu', laplace_kernel.astype(jnp.float32), residual.astype(jnp.float32))
        rounded = lax.optimization_barrier(subtotal_sums.astype(jnp.bfloat16))
        return (running, step_rate * lax.optimization_barrier(jnp.sum(rounded.astype(jnp.float32), axis=0)))
    _, grads = lax.scan(gradient, jnp.zeros((), jnp.float32), center_blocks)
    grad = grads.reshape(N_CENTER * PC, C)
    picked = jnp.take(grad, subset_index.astype(jnp.int32), axis=0).astype(jnp.bfloat16)
    projected = lax.dot_general(basis, picked, (((0,), (0,)), ((), ())), preferred_element_type=jnp.float32)
    scaled = (damping[:, None] * projected).astype(jnp.bfloat16)
    correction = jnp.dot(basis, scaled, preferred_element_type=jnp.float32)
    updated = (weights.astype(jnp.float32) - grad).at[subset_index.astype(jnp.int32)].add(correction)
    return (updated.astype(jnp.bfloat16), residual)
```

```python
import jax
import jax.numpy as jnp
from jax import lax
from jax.sharding import Mesh, PartitionSpec as P

kernel_length = 2.0
step_rate = 0.1
f32 = jnp.float32
bf16 = jnp.bfloat16


def exchange(values, axes):
    return lax.all_to_all(values, axes, split_axis=0, concat_axis=0, tiled=True)


def rows_dot(left, right):
    return lax.dot_general(left, right, (((0,), (0,)), ((), ())), preferred_element_type=f32)


def laplace(features, centers, centers_sq):
    sample_sq = jnp.sum(jnp.square(features.astype(f32)), axis=1)
    cross = lax.dot_general(
        features, centers, (((1,), (1,)), ((), ())), preferred_element_type=f32
    )
    distance = sample_sq[:, None] + centers_sq[None, :] - 2.0 * cross
    return jnp.exp(-jnp.sqrt(jnp.maximum(distance, 0.0)) / kernel_length).astype(bf16)


def pick_row(stored, picks):
    lanes = lax.broadcasted_iota(jnp.int32, (picks.shape[0], stored.shape[0]), 1)
    return jnp.dot(
        (picks[:, None] == lanes).astype(bf16), stored, preferred_element_type=f32
    ).astype(bf16)


def per_device(
    centers, weights, subset_index, basis, damping, stored_train_features, pool_labels, picks
):
    nx, nz, nc, ny = (lax.axis_size(a) for a in ("x", "z", "core", "batch"))
    devices = nx * nz * nc
    own_rows = picks.shape[1]
    center_rows, width = centers.shape
    outputs = weights.shape[1]
    entries, eigen = basis.shape
    capacity = 4 * entries // devices
    block = nz * own_rows
    group = lax.axis_index("batch")
    core = lax.axis_index("core")

    own_features = pick_row(stored_train_features[0], picks[0])

    holder = subset_index // center_rows
    local_row = subset_index - holder * center_rows
    order = lax.iota(jnp.int32, entries)
    same_holder = holder[:, None] == holder[None, :]
    rank = jnp.sum((same_holder & (order[:, None] > order[None, :])).astype(jnp.int32), axis=1)
    lane = lax.broadcasted_iota(jnp.int32, (entries, eigen), 1)
    digit = jnp.where(lane % 2 == 0, (local_row % 256)[:, None], (local_row // 256)[:, None])
    position = jnp.where(lane // 2 == rank[:, None], digit, 0).astype(bf16)
    carried = jnp.where(
        group < capacity, jnp.where((rank == group)[:, None], basis, 0), position
    )
    column = holder // (nz * nc)
    spread = jnp.concatenate(
        [jnp.where((column == k)[:, None], carried, 0) for k in range(nx)], axis=1
    )
    goal = lax.broadcasted_iota(jnp.int32, (nz * nc, entries), 0)
    slots = jnp.dot(
        (goal == (holder % (nz * nc))[None, :]).astype(bf16), spread, preferred_element_type=f32
    ).astype(bf16)
    first = jnp.concatenate(
        [
            jnp.broadcast_to(own_features[None], (nz, own_rows, width)),
            slots.reshape(nz, nc, nx * eigen),
        ],
        axis=2,
    )
    first = exchange(first, "z").reshape(block, width + nx * eigen)
    second = jnp.stack(
        [
            jnp.concatenate(
                [first[:, :width], first[:, width + k * eigen : width + (k + 1) * eigen]], axis=1
            )
            for k in range(nx)
        ]
    )
    second = jnp.broadcast_to(second[None], (ny, nx, block, width + eigen))
    second = exchange(second.reshape(ny * nx, block, width + eigen), ("batch", "x"))
    features = lax.all_gather(second[:, :, :width], "core").reshape(nc, ny, nx * block, width)
    packed = lax.all_gather(second[:, :, width:], "core").reshape(nc, ny, nx * block, eigen)

    digits = packed[:, capacity].astype(f32)
    parity = lax.broadcasted_iota(jnp.int32, (nc, nx * block), 1) % nc
    places = jnp.stack(
        [
            jnp.where(
                parity == core, digits[:, :, 2 * k] + 256.0 * digits[:, :, 2 * k + 1], -1.0
            )
            for k in range(capacity)
        ],
        axis=1,
    ).astype(jnp.int32)
    places = places.reshape(nc * capacity * nx * block, 1)
    member = (
        places == lax.broadcasted_iota(jnp.int32, (places.shape[0], center_rows), 1)
    ).astype(bf16)
    local_basis = rows_dot(
        member, packed[:, :capacity].reshape(nc * capacity * nx * block, eigen)
    ).astype(bf16)

    centers_sq = jnp.sum(jnp.square(centers.astype(f32)), axis=1)
    own_group = lax.dynamic_index_in_dim(features, group, 1, keepdims=False)
    own_kernel = laplace(own_group.reshape(nc * nx * block, width), centers, centers_sq)
    partial = jnp.dot(
        own_kernel, jnp.concatenate([weights, local_basis], axis=1), preferred_element_type=f32
    ).astype(bf16)
    wide = outputs + eigen
    partial = exchange(partial.reshape(nc * nx, block, wide), ("core", "x"))
    partial = jnp.sum(partial.astype(f32), axis=0).astype(bf16)
    partial = exchange(partial.reshape(nz, own_rows, wide), "z")
    total = jnp.sum(partial.astype(f32), axis=0)
    own_targets = pick_row(pool_labels[0], picks[0])
    residual = (total[:, :outputs] - own_targets.astype(f32)).astype(bf16)
    own = jnp.concatenate([residual, total[:, outputs:].astype(bf16)], axis=1)

    own = exchange(jnp.broadcast_to(own[None], (nz, own_rows, wide)), "z")
    own = jnp.broadcast_to(own.reshape(1, block, wide), (ny * nx, block, wide))
    here = exchange(own, ("batch", "x")).reshape(ny * nx * block, wide)
    there = lax.ppermute(here, "core", [(k, nc - 1 - k) for k in range(nc)])

    features = features.reshape(nc, ny * nx * block, width)
    kernel_here = laplace(
        lax.dynamic_index_in_dim(features, core, 0, keepdims=False), centers, centers_sq
    )
    kernel_there = laplace(
        lax.dynamic_index_in_dim(features, nc - 1 - core, 0, keepdims=False), centers, centers_sq
    )
    projected = rows_dot(here[:, outputs:], here[:, :outputs]) + rows_dot(
        there[:, outputs:], there[:, :outputs]
    )
    scaled = (damping[:, None] * projected).astype(bf16)
    gradient = rows_dot(kernel_here, here[:, :outputs]) + rows_dot(
        kernel_there, there[:, :outputs]
    )
    change = gradient - jnp.dot(local_basis, scaled, preferred_element_type=f32)
    updated = (weights.astype(f32) - step_rate * change).astype(bf16)
    return (updated, residual[None])


def solution(mesh):
    devices = mesh.devices
    fine = Mesh(
        devices.reshape(4, devices.shape[0] // 8, 2, devices.shape[1]),
        ("x", "z", "core", "batch"),
    )
    center = ("x", "z", "core")
    return jax.shard_map(
        per_device,
        mesh=fine,
        in_specs=(
            P(center, None),
            P(center, None),
            P(center),
            P(center, None),
            P(),
            P("batch", center, None),
            P("batch", center, None),
            P("batch", center),
        ),
        out_specs=(P(center, None), P("batch", center, None)),
        check_vma=False,
    )
```

```python
import functools

import jax
import jax.numpy as jnp
from jax import lax
from jax.experimental import pallas as pl
from jax.experimental.pallas import tpu as pltpu
from jax.sharding import Mesh, PartitionSpec as P

kernel_length = 2.0
step_rate = 0.1
f32 = jnp.float32
bf16 = jnp.bfloat16
i32 = jnp.int32
VMEM = pltpu.VMEM


def exchange(values, axes):
    return lax.all_to_all(values, axes, split_axis=0, concat_axis=0, tiled=True)


def iota(shape, dim):
    return lax.broadcasted_iota(i32, shape, dim)


def mxu(left, right, contract=((1,), (0,))):
    return lax.dot_general(left, right, (contract, ((), ())), preferred_element_type=f32)


def rows_dot(left, right):
    return mxu(left, right, ((0,), (0,)))


def laplace(distance):
    return jnp.exp(-jnp.sqrt(jnp.maximum(distance, 0.0)) / kernel_length).astype(bf16)


def prepare(sizes, *refs):
    nx, nz, nc, rows_each, capacity = sizes
    out_ref, target_ref = refs[5:7]
    picks_ref, index_ref, basis_ref, stored_ref, label_ref, done = refs[7:]
    copies = [
        pltpu.make_async_copy(source, target, done.at[k])
        for k, (source, target) in enumerate(zip(refs[:5], refs[7:12]))
    ]
    for copy in copies:
        copy.start()
    for copy in copies:
        copy.wait()
    entries, eigen = basis_ref.shape
    group = lax.axis_index("batch")
    upper = jnp.where(lax.axis_index("x") < nx // 2, 0, eigen // 8)
    half = eigen // 2
    depth, width = stored_ref.shape
    index = index_ref[...]
    eye = iota((entries, entries), 0) == iota((entries, entries), 1)
    bits = rows_each.bit_length() - 1
    holder = lax.shift_right_logical(index, bits)
    column = jnp.sum(jnp.where(eye, index, 0), axis=1, keepdims=True)
    column_holder = lax.shift_right_logical(column, bits)
    column_row = lax.bitwise_and(column, rows_each - 1)
    earlier = iota((entries, entries), 0) > iota((entries, entries), 1)
    rank = jnp.sum(
        jnp.where((column_holder == holder) & earlier, 1, 0), axis=1, keepdims=True
    )
    lane = lax.bitwise_and(iota((entries, eigen), 1), half - 1)
    low = lax.bitwise_and(column_row, 255)
    high = lax.shift_right_logical(column_row, 8)
    digit = jnp.where(lax.bitwise_and(lane, 1) == 0, low, high)
    position = jnp.where(lax.shift_right_logical(lane, 1) == rank + upper, digit, 0).astype(f32)
    kept = jnp.where(rank == group, basis_ref[...].astype(f32), 0.0)
    carried = jnp.where(group < capacity, kept, position)
    carried = jnp.concatenate([carried[:, :half], carried[:, half:]], axis=0)
    line_bits = (nz * nc).bit_length() - 1
    corner = lax.shift_right_logical(column_holder, line_bits) * nc + lax.bitwise_and(
        column_holder, nc - 1
    )
    corner = jnp.concatenate([corner, corner], axis=0)
    line = lax.shift_right_logical(lax.bitwise_and(holder, nz * nc - 1), nc.bit_length() - 1)
    here = iota((2 * nz, entries), 0)
    same = lax.shift_right_logical(here, 1) == line
    odd = lax.bitwise_and(here, 1)
    goal = jnp.concatenate(
        [jnp.where(same & (odd == h), 1.0, 0.0).astype(bf16) for h in range(2)], axis=1
    )
    sample = iota((2 * nz, depth), 0)
    wanted = jnp.where(lax.bitwise_and(sample, 1) == 0, picks_ref[0, 0], picks_ref[0, 1])
    picked = jnp.where(wanted == iota((2 * nz, depth), 1), 1.0, 0.0).astype(bf16)
    out_ref[:, :width] = mxu(picked, stored_ref[...]).astype(bf16)
    target_ref[...] = mxu(picked[: target_ref.shape[0], :], label_ref[...])
    for k in range(nx * nc):
        spread = jnp.where(corner == k, carried, 0.0).astype(bf16)
        out_ref[:, width + k * half : width + (k + 1) * half] = mxu(goal, spread).astype(bf16)


def squares(values):
    wide = values.astype(f32)
    return jnp.sum(wide * wide, axis=1, keepdims=True)


def as_row(column):
    return jnp.broadcast_to(column, (column.shape[0], 128)).T[:1, :]


def predict(sizes, place_ref, features_ref, kept_ref, pair_ref, centers_ref, weights_ref, *outs):
    nc, ny, capacity = sizes
    out_ref, basis_ref = outs
    core, group = place_ref[0], place_ref[1]
    other = nc - 1 - core
    count, width = features_ref.shape
    rows = centers_ref.shape[0]
    outputs = weights_ref.shape[1]
    side = count // ny
    parts = width // 128
    centers = centers_ref[...]
    line = as_row(squares(centers))

    def across(features):
        cross = mxu(features, centers, ((1,), (1,)))
        return laplace(squares(features) + line - 2.0 * cross)

    start = pl.multiple_of(group * side, side)
    near = across(features_ref[pl.ds(start, side), :])
    far = across(
        jnp.concatenate(
            [
                pair_ref[other, pl.ds(pl.multiple_of(k * count + start, side), side), :]
                for k in range(parts)
            ],
            axis=1,
        )
    )

    at = iota((rows, side), 0)
    parity = lax.bitwise_and(iota((1, side), 1), 1)
    halves = [jnp.zeros((rows, 128), f32) for _ in range(2)]
    for c in range(2):
        if c == 0:
            blocks = [kept_ref[k * side : (k + 1) * side, :] for k in range(capacity)]
            digits = kept_ref[capacity * side :, :]
        else:
            first = parts * count
            blocks = [
                pair_ref[other, first + k * side : first + (k + 1) * side, :]
                for k in range(capacity)
            ]
            digits = pair_ref[other, first + capacity * side :, :]
        digits = digits.astype(f32)
        digits = jnp.concatenate([digits, digits], axis=0).T
        for k in range(capacity):
            low, high = (
                digits[2 * k + d : 2 * k + d + 1, :] + 256.0 * digits[2 * k + d + 1 : 2 * k + d + 2, :]
                for d in (0, 64)
            )
            place = jnp.where(iota((1, side), 1) < side // 2, low, high).astype(i32)
            for h in range(2):
                held = jnp.where(parity == h, place, -1)
                member = jnp.where(at == held, 1.0, 0.0).astype(bf16)
                halves[h] = halves[h] + mxu(member, blocks[k])
    local = jnp.concatenate(halves, axis=1).astype(bf16)
    basis_ref[...] = local
    for kernel, to in ((near, core), (far, other)):
        spot = pl.ds(pl.multiple_of(to * side, side), side)
        out_ref[spot, :outputs] = mxu(kernel, weights_ref[...]).astype(bf16)
        out_ref[spot, outputs:] = mxu(kernel, local).astype(bf16)


def spread(place_ref, features_ref, pair_ref, centers_ref, here_ref, there_ref):
    other = 1 - place_ref[0]
    count, width = features_ref.shape
    centers = centers_ref[...]
    column = squares(centers)
    theirs = jnp.concatenate(
        [pair_ref[other, k * count : (k + 1) * count, :] for k in range(width // 128)], axis=1
    )
    for out_ref, features in ((here_ref, features_ref[...]), (there_ref, theirs)):
        cross = mxu(centers, features, ((1,), (1,)))
        out_ref[...] = laplace(column + as_row(squares(features)) - 2.0 * cross)


def begin(kernel_hbm, damping_hbm, here_ref, *refs):
    slope_ref, project_ref, column_ref, kernel_ref, damping_ref, done = refs
    outputs = slope_ref.shape[1]
    copies = [
        pltpu.make_async_copy(kernel_hbm, kernel_ref, done.at[0]),
        pltpu.make_async_copy(damping_hbm, damping_ref, done.at[1]),
    ]
    for copy in copies:
        copy.start()
    project_ref[...] = rows_dot(here_ref[:, outputs:], here_ref[:, :outputs])
    for copy in copies:
        copy.wait()
    slope_ref[...] = mxu(kernel_ref[...], here_ref[:, :outputs])
    row = damping_ref[...]
    column_ref[...] = jnp.broadcast_to(row, (128, row.shape[1])).T[:, :1]


def update(steps, kernel_ref, there_ref, slope_ref, project_ref, basis_ref, damping_ref, weights_ref, out_hbm, held, done):
    rows, outputs = weights_ref.shape
    total = project_ref[...] + rows_dot(there_ref[:, outputs:], there_ref[:, :outputs])
    scaled = (damping_ref[...] * total).astype(bf16)
    tall = rows // steps
    copies = []
    for k in range(steps):
        at = slice(k * tall, (k + 1) * tall)
        change = slope_ref[at, :] + mxu(kernel_ref[at, :], there_ref[:, :outputs])
        change = change - mxu(basis_ref[at, :], scaled)
        held[at, :] = (weights_ref[at, :].astype(f32) - step_rate * change).astype(bf16)
        copy = pltpu.make_async_copy(held.at[at, :], out_hbm.at[at, :], done.at[k])
        copy.start()
        copies.append(copy)
    for copy in copies:
        copy.wait()


def per_device(
    centers, weights, subset_index, basis, damping, stored_train_features, pool_labels, picks
):
    nx, nz, nc, ny = (lax.axis_size(a) for a in ("x", "z", "core", "batch"))
    devices = nx * nz * nc
    own_rows = picks.shape[1]
    center_rows, width = centers.shape
    outputs = weights.shape[1]
    entries, eigen = basis.shape
    capacity = 4 * entries // devices
    block = nz * own_rows
    side = nx * block
    wide = outputs + eigen
    half = eigen // 2
    group = lax.axis_index("batch")
    core = lax.axis_index("core")
    smem = pl.BlockSpec(memory_space=pltpu.SMEM)
    vmem = pl.BlockSpec(memory_space=VMEM)
    hbm = pl.BlockSpec(memory_space=pltpu.HBM)
    small = pltpu.CompilerParams(vmem_limit_bytes=16 * 1024 * 1024)

    first, own_targets = pl.pallas_call(
        functools.partial(prepare, (nx, nz, nc, center_rows, capacity)),
        out_shape=(
            jax.ShapeDtypeStruct((block, width + nx * eigen), bf16),
            jax.ShapeDtypeStruct((min(8, block), outputs), f32),
        ),
        in_specs=[hbm] * 5,
        out_specs=(vmem, vmem),
        scratch_shapes=[
            pltpu.SMEM((1, own_rows), i32),
            VMEM((1, entries), i32),
            VMEM((entries, eigen), bf16),
            VMEM(stored_train_features.shape[1:], bf16),
            VMEM(pool_labels.shape[1:], bf16),
            pltpu.SemaphoreType.DMA((5,)),
        ],
        compiler_params=small,
    )(
        *(
            pltpu.with_memory_space_constraint(v, pltpu.HBM)
            for v in (
                picks,
                subset_index.reshape(1, entries),
                basis,
                stored_train_features[0],
                pool_labels[0],
            )
        )
    )
    first = first.reshape(nz, own_rows, width + nx * eigen)
    first, group, core = lax.optimization_barrier((first, group, core))
    first = exchange(first, "z").reshape(block, width + nx * eigen)
    second = jnp.stack(
        [
            jnp.concatenate(
                [first[:, :width], first[:, width + k * eigen : width + (k + 1) * eigen]], axis=1
            )
            for k in range(nx)
        ]
    )
    second = jnp.broadcast_to(second[None], (ny, nx, block, width + eigen))
    second, group, core = lax.optimization_barrier((second, group, core))
    second = exchange(second.reshape(ny * nx, block, width + eigen), ("batch", "x"))
    second, group, core = lax.optimization_barrier((second, group, core))
    features = second[:, :, :width].reshape(ny * side, width)
    near = second[:, :, width : width + half].reshape(ny * side, half)
    far = second[:, :, width + half :].reshape(ny * side, half)
    kept, sent = jnp.where(core == 0, near, far), jnp.where(core == 0, far, near)
    places = capacity * side
    kept, sent = (
        jnp.concatenate([v[:places], v[places : places + side // 2] + v[places + side // 2 :]])
        for v in (kept, sent)
    )
    pair = lax.all_gather(
        jnp.concatenate(
            [features[:, k : k + 128] for k in range(0, width, 128)] + [sent], axis=0
        ),
        "core",
    )
    place = jnp.stack([core, group])
    partial, local_basis = pl.pallas_call(
        functools.partial(predict, (nc, ny, capacity)),
        out_shape=(
            jax.ShapeDtypeStruct((nc * side, wide), bf16),
            jax.ShapeDtypeStruct((center_rows, eigen), bf16),
        ),
        in_specs=[smem, vmem, vmem, vmem, vmem, vmem],
        out_specs=(vmem, vmem),
        compiler_params=small,
    )(place, features, kept, pair, centers, weights)
    partial = exchange(partial.reshape(nc * nx, block, wide), ("core", "x"))
    partial = jnp.sum(partial.astype(f32), axis=0).astype(bf16)
    partial, place = lax.optimization_barrier((partial, place))
    partial = exchange(partial.reshape(nz, own_rows, wide), "z")
    square = jax.ShapeDtypeStruct((center_rows, ny * side), bf16)
    kernel_here, kernel_there = pl.pallas_call(
        spread,
        out_shape=(square, square),
        in_specs=[smem, vmem, vmem, vmem],
        out_specs=(vmem, vmem),
        compiler_params=small,
    )(place, features, pair, centers)
    total = jnp.sum(partial.astype(f32), axis=0)
    residual = (total[:, :outputs] - own_targets[:own_rows]).astype(bf16)
    own = jnp.concatenate([residual, total[:, outputs:].astype(bf16)], axis=1)
    own, kernel_here, kernel_there = lax.optimization_barrier((own, kernel_here, kernel_there))

    own_all = exchange(jnp.broadcast_to(own[None], (nz, own_rows, wide)), "z")
    own_all = jnp.broadcast_to(own_all.reshape(1, block, wide), (ny * nx, block, wide))
    here = exchange(own_all, ("batch", "x"))
    residual = lax.dynamic_slice(
        here,
        (group * nx + lax.axis_index("x"), lax.axis_index("z") * own_rows, 0),
        (1, own_rows, outputs),
    )
    here = here.reshape(ny * side, wide)
    there = lax.ppermute(here, "core", [(k, nc - 1 - k) for k in range(nc)])
    slope, projected, damping = pl.pallas_call(
        begin,
        out_shape=(
            jax.ShapeDtypeStruct((center_rows, outputs), f32),
            jax.ShapeDtypeStruct((eigen, outputs), f32),
            jax.ShapeDtypeStruct((eigen, 1), f32),
        ),
        in_specs=[hbm, hbm, vmem],
        out_specs=(vmem, vmem, vmem),
        scratch_shapes=[
            VMEM(kernel_here.shape, bf16),
            VMEM((1, eigen), f32),
            pltpu.SemaphoreType.DMA((2,)),
        ],
        compiler_params=small,
    )(
        pltpu.with_memory_space_constraint(kernel_here, pltpu.HBM),
        pltpu.with_memory_space_constraint(damping.reshape(1, eigen), pltpu.HBM),
        here,
    )
    steps = 4
    updated = pl.pallas_call(
        functools.partial(update, steps),
        out_shape=jax.ShapeDtypeStruct((center_rows, outputs), bf16),
        in_specs=[vmem] * 7,
        out_specs=hbm,
        scratch_shapes=[
            VMEM((center_rows, outputs), bf16),
            pltpu.SemaphoreType.DMA((steps,)),
        ],
        compiler_params=small,
    )(kernel_there, there, slope, projected, local_basis, damping, weights)
    return (updated, residual)


def solution(mesh):
    devices = mesh.devices
    fine = Mesh(
        devices.reshape(4, devices.shape[0] // 8, 2, devices.shape[1]),
        ("x", "z", "core", "batch"),
    )
    center = ("x", "z", "core")
    return jax.shard_map(
        per_device,
        mesh=fine,
        in_specs=(
            P(center, None),
            P(center, None),
            P(center),
            P(center, None),
            P(),
            P("batch", center, None),
            P("batch", center, None),
            P("batch", center),
        ),
        out_specs=(P(center, None), P("batch", center, None)),
        check_vma=False,
    )
```

```python
import functools

import jax
import jax.numpy as jnp
from jax import lax
from jax.experimental import pallas as pl
from jax.experimental.pallas import tpu as pltpu
from jax.sharding import Mesh, PartitionSpec as P

kernel_length = 2.0
step_rate = 0.1
f32 = jnp.float32
bf16 = jnp.bfloat16
i32 = jnp.int32
VMEM = pltpu.VMEM


def far_first(size):
    return [(k + size // 2) % size for k in range(size)]


def exchange(values, *axes):
    order = [0]
    for axis in axes:
        size = lax.axis_size(axis)
        own = range(size) if axis == "core" else far_first(size)
        order = [k * size + j for k in order for j in own]
    names = axes if len(axes) > 1 else axes[0]
    return lax.all_to_all(
        values, names, split_axis=0, concat_axis=0, tiled=True, axis_index_groups=[order]
    )


def spot(axis):
    size = lax.axis_size(axis)
    return lax.rem(lax.axis_index(axis) + size // 2, size)


def iota(shape, dim):
    return lax.broadcasted_iota(i32, shape, dim)


def mxu(left, right, contract=((1,), (0,))):
    return lax.dot_general(left, right, (contract, ((), ())), preferred_element_type=f32)


def rows_dot(left, right):
    return mxu(left, right, ((0,), (0,)))


def laplace(distance):
    return jnp.exp(-jnp.sqrt(jnp.maximum(distance, 0.0)) / kernel_length).astype(bf16)


def prepare(sizes, *refs):
    nx, nz, nc, rows_each, capacity = sizes
    out_ref, target_ref = refs[5:7]
    picks_ref, index_ref, basis_ref, stored_ref, label_ref, done = refs[7:]
    copies = [
        pltpu.make_async_copy(source, target, done.at[k])
        for k, (source, target) in enumerate(zip(refs[:5], refs[7:12]))
    ]
    for copy in copies:
        copy.start()
    for copy in copies:
        copy.wait()
    entries, eigen = basis_ref.shape
    group = spot("batch")
    upper = jnp.where(spot("x") < nx // 2, 0, eigen // 8)
    half = eigen // 2
    depth, width = stored_ref.shape
    index = index_ref[...]
    eye = iota((entries, entries), 0) == iota((entries, entries), 1)
    bits = rows_each.bit_length() - 1
    holder = lax.shift_right_logical(index, bits)
    column = jnp.sum(jnp.where(eye, index, 0), axis=1, keepdims=True)
    column_holder = lax.shift_right_logical(column, bits)
    column_row = lax.bitwise_and(column, rows_each - 1)
    earlier = iota((entries, entries), 0) > iota((entries, entries), 1)
    rank = jnp.sum(
        jnp.where((column_holder == holder) & earlier, 1, 0), axis=1, keepdims=True
    )
    lane = lax.bitwise_and(iota((entries, eigen), 1), half - 1)
    low = lax.bitwise_and(column_row, 255)
    high = lax.shift_right_logical(column_row, 8)
    digit = jnp.where(lax.bitwise_and(lane, 1) == 0, low, high)
    position = jnp.where(lax.shift_right_logical(lane, 1) == rank + upper, digit, 0).astype(f32)
    kept = jnp.where(rank == group, basis_ref[...].astype(f32), 0.0)
    carried = jnp.where(group < capacity, kept, position)
    carried = jnp.concatenate([carried[:, :half], carried[:, half:]], axis=0)
    line_bits = (nz * nc).bit_length() - 1
    across = lax.shift_right_logical(column_holder, line_bits)
    across = lax.bitwise_and(across + nx // 2, nx - 1)
    corner = across * nc + lax.bitwise_and(column_holder, nc - 1)
    corner = jnp.concatenate([corner, corner], axis=0)
    line = lax.shift_right_logical(lax.bitwise_and(holder, nz * nc - 1), nc.bit_length() - 1)
    line = lax.bitwise_and(line + nz // 2, nz - 1)
    here = iota((2 * nz, entries), 0)
    same = lax.shift_right_logical(here, 1) == line
    odd = lax.bitwise_and(here, 1)
    goal = jnp.concatenate(
        [jnp.where(same & (odd == h), 1.0, 0.0).astype(bf16) for h in range(2)], axis=1
    )
    sample = iota((2 * nz, depth), 0)
    wanted = jnp.where(lax.bitwise_and(sample, 1) == 0, picks_ref[0, 0], picks_ref[0, 1])
    picked = jnp.where(wanted == iota((2 * nz, depth), 1), 1.0, 0.0).astype(bf16)
    out_ref[:, :width] = mxu(picked, stored_ref[...]).astype(bf16)
    target_ref[...] = mxu(picked[: target_ref.shape[0], :], label_ref[...])
    for k in range(nx * nc):
        spread = jnp.where(corner == k, carried, 0.0).astype(bf16)
        out_ref[:, width + k * half : width + (k + 1) * half] = mxu(goal, spread).astype(bf16)


def squares(values):
    wide = values.astype(f32)
    return jnp.sum(wide * wide, axis=1, keepdims=True)


def as_row(column):
    return jnp.broadcast_to(column, (column.shape[0], 128)).T[:1, :]


def predict(sizes, place_ref, features_ref, kept_ref, pair_ref, centers_ref, weights_ref, *outs):
    nc, ny, capacity = sizes
    out_ref, basis_ref = outs
    core, group = place_ref[0], place_ref[1]
    other = nc - 1 - core
    count, width = features_ref.shape
    rows = centers_ref.shape[0]
    outputs = weights_ref.shape[1]
    side = count // ny
    parts = width // 128
    centers = centers_ref[...]
    line = as_row(squares(centers))

    def across(features):
        cross = mxu(features, centers, ((1,), (1,)))
        return laplace(squares(features) + line - 2.0 * cross)

    start = pl.multiple_of(group * side, side)
    near = across(features_ref[pl.ds(start, side), :])
    far = across(
        jnp.concatenate(
            [
                pair_ref[other, pl.ds(pl.multiple_of(k * count + start, side), side), :]
                for k in range(parts)
            ],
            axis=1,
        )
    )

    at = iota((rows, side), 0)
    parity = lax.bitwise_and(iota((1, side), 1), 1)
    halves = [jnp.zeros((rows, 128), f32) for _ in range(2)]
    for c in range(2):
        if c == 0:
            blocks = [kept_ref[k * side : (k + 1) * side, :] for k in range(capacity)]
            digits = kept_ref[capacity * side :, :]
        else:
            first = parts * count
            blocks = [
                pair_ref[other, first + k * side : first + (k + 1) * side, :]
                for k in range(capacity)
            ]
            digits = pair_ref[other, first + capacity * side :, :]
        digits = digits.astype(f32)
        digits = jnp.concatenate([digits, digits], axis=0).T
        for k in range(capacity):
            low, high = (
                digits[2 * k + d : 2 * k + d + 1, :] + 256.0 * digits[2 * k + d + 1 : 2 * k + d + 2, :]
                for d in (0, 64)
            )
            place = jnp.where(iota((1, side), 1) < side // 2, low, high).astype(i32)
            for h in range(2):
                held = jnp.where(parity == h, place, -1)
                member = jnp.where(at == held, 1.0, 0.0).astype(bf16)
                halves[h] = halves[h] + mxu(member, blocks[k])
    local = jnp.concatenate(halves, axis=1).astype(bf16)
    basis_ref[...] = local
    for kernel, to in ((near, core), (far, other)):
        spot = pl.ds(pl.multiple_of(to * side, side), side)
        out_ref[spot, :outputs] = mxu(kernel, weights_ref[...]).astype(bf16)
        out_ref[spot, outputs:] = mxu(kernel, local).astype(bf16)


def spread(place_ref, features_ref, pair_ref, centers_ref, here_ref, there_ref):
    other = 1 - place_ref[0]
    count, width = features_ref.shape
    centers = centers_ref[...]
    column = squares(centers)
    theirs = jnp.concatenate(
        [pair_ref[other, k * count : (k + 1) * count, :] for k in range(width // 128)], axis=1
    )
    for out_ref, features in ((here_ref, features_ref[...]), (there_ref, theirs)):
        cross = mxu(centers, features, ((1,), (1,)))
        out_ref[...] = laplace(column + as_row(squares(features)) - 2.0 * cross)


def begin(kernel_hbm, damping_hbm, here_ref, *refs):
    slope_ref, project_ref, column_ref, kernel_ref, damping_ref, done = refs
    outputs = slope_ref.shape[1]
    copies = [
        pltpu.make_async_copy(kernel_hbm, kernel_ref, done.at[0]),
        pltpu.make_async_copy(damping_hbm, damping_ref, done.at[1]),
    ]
    for copy in copies:
        copy.start()
    project_ref[...] = rows_dot(here_ref[:, outputs:], here_ref[:, :outputs])
    for copy in copies:
        copy.wait()
    slope_ref[...] = mxu(kernel_ref[...], here_ref[:, :outputs])
    row = damping_ref[...]
    column_ref[...] = jnp.broadcast_to(row, (128, row.shape[1])).T[:, :1]


def update(steps, kernel_ref, there_ref, slope_ref, project_ref, basis_ref, damping_ref, weights_ref, out_hbm, held, done):
    rows, outputs = weights_ref.shape
    total = project_ref[...] + rows_dot(there_ref[:, outputs:], there_ref[:, :outputs])
    scaled = (damping_ref[...] * total).astype(bf16)
    tall = rows // steps
    copies = []
    for k in range(steps):
        at = slice(k * tall, (k + 1) * tall)
        change = slope_ref[at, :] + mxu(kernel_ref[at, :], there_ref[:, :outputs])
        change = change - mxu(basis_ref[at, :], scaled)
        held[at, :] = (weights_ref[at, :].astype(f32) - step_rate * change).astype(bf16)
        copy = pltpu.make_async_copy(held.at[at, :], out_hbm.at[at, :], done.at[k])
        copy.start()
        copies.append(copy)
    for copy in copies:
        copy.wait()


def per_device(
    centers, weights, subset_index, basis, damping, stored_train_features, pool_labels, picks
):
    nx, nz, nc, ny = (lax.axis_size(a) for a in ("x", "z", "core", "batch"))
    devices = nx * nz * nc
    own_rows = picks.shape[1]
    center_rows, width = centers.shape
    outputs = weights.shape[1]
    entries, eigen = basis.shape
    capacity = 4 * entries // devices
    block = nz * own_rows
    side = nx * block
    wide = outputs + eigen
    half = eigen // 2
    group = spot("batch")
    core = lax.axis_index("core")
    smem = pl.BlockSpec(memory_space=pltpu.SMEM)
    vmem = pl.BlockSpec(memory_space=VMEM)
    hbm = pl.BlockSpec(memory_space=pltpu.HBM)
    small = pltpu.CompilerParams(vmem_limit_bytes=16 * 1024 * 1024)

    first, own_targets = pl.pallas_call(
        functools.partial(prepare, (nx, nz, nc, center_rows, capacity)),
        out_shape=(
            jax.ShapeDtypeStruct((block, width + nx * eigen), bf16),
            jax.ShapeDtypeStruct((min(8, block), outputs), f32),
        ),
        in_specs=[hbm] * 5,
        out_specs=(vmem, vmem),
        scratch_shapes=[
            pltpu.SMEM((1, own_rows), i32),
            VMEM((1, entries), i32),
            VMEM((entries, eigen), bf16),
            VMEM(stored_train_features.shape[1:], bf16),
            VMEM(pool_labels.shape[1:], bf16),
            pltpu.SemaphoreType.DMA((5,)),
        ],
        compiler_params=small,
    )(
        *(
            pltpu.with_memory_space_constraint(v, pltpu.HBM)
            for v in (
                picks,
                subset_index.reshape(1, entries),
                basis,
                stored_train_features[0],
                pool_labels[0],
            )
        )
    )
    first = first.reshape(nz, own_rows, width + nx * eigen)
    first, group, core = lax.optimization_barrier((first, group, core))
    first = exchange(first, "z").reshape(block, width + nx * eigen)
    second = jnp.stack(
        [
            jnp.concatenate(
                [first[:, :width], first[:, width + k * eigen : width + (k + 1) * eigen]], axis=1
            )
            for k in range(nx)
        ]
    )
    second = jnp.broadcast_to(second[None], (ny, nx, block, width + eigen))
    second, group, core = lax.optimization_barrier((second, group, core))
    second = exchange(second.reshape(ny * nx, block, width + eigen), "batch", "x")
    second, group, core = lax.optimization_barrier((second, group, core))
    features = second[:, :, :width].reshape(ny * side, width)
    near = second[:, :, width : width + half].reshape(ny * side, half)
    far = second[:, :, width + half :].reshape(ny * side, half)
    kept, sent = jnp.where(core == 0, near, far), jnp.where(core == 0, far, near)
    places = capacity * side
    kept, sent = (
        jnp.concatenate([v[:places], v[places : places + side // 2] + v[places + side // 2 :]])
        for v in (kept, sent)
    )
    pair = lax.all_gather(
        jnp.concatenate(
            [features[:, k : k + 128] for k in range(0, width, 128)] + [sent], axis=0
        ),
        "core",
    )
    place = jnp.stack([core, group])
    partial, local_basis = pl.pallas_call(
        functools.partial(predict, (nc, ny, capacity)),
        out_shape=(
            jax.ShapeDtypeStruct((nc * side, wide), bf16),
            jax.ShapeDtypeStruct((center_rows, eigen), bf16),
        ),
        in_specs=[smem, vmem, vmem, vmem, vmem, vmem],
        out_specs=(vmem, vmem),
        compiler_params=small,
    )(place, features, kept, pair, centers, weights)
    partial = exchange(partial.reshape(nc * nx, block, wide), "core", "x")
    partial = jnp.sum(partial.astype(f32), axis=0).astype(bf16)
    partial, place = lax.optimization_barrier((partial, place))
    partial = exchange(partial.reshape(nz, own_rows, wide), "z")
    square = jax.ShapeDtypeStruct((center_rows, ny * side), bf16)
    kernel_here, kernel_there = pl.pallas_call(
        spread,
        out_shape=(square, square),
        in_specs=[smem, vmem, vmem, vmem],
        out_specs=(vmem, vmem),
        compiler_params=small,
    )(place, features, pair, centers)
    total = jnp.sum(partial.astype(f32), axis=0)
    residual = (total[:, :outputs] - own_targets[:own_rows]).astype(bf16)
    own = jnp.concatenate([residual, total[:, outputs:].astype(bf16)], axis=1)
    own, kernel_here, kernel_there = lax.optimization_barrier((own, kernel_here, kernel_there))

    own_all = exchange(jnp.broadcast_to(own[None], (nz, own_rows, wide)), "z")
    own_all = jnp.broadcast_to(own_all.reshape(1, block, wide), (ny * nx, block, wide))
    here = exchange(own_all, "batch", "x")
    residual = lax.dynamic_slice(
        here,
        (spot("batch") * nx + spot("x"), spot("z") * own_rows, 0),
        (1, own_rows, outputs),
    )
    here = here.reshape(ny * side, wide)
    there = lax.ppermute(here, "core", [(k, nc - 1 - k) for k in range(nc)])
    slope, projected, damping = pl.pallas_call(
        begin,
        out_shape=(
            jax.ShapeDtypeStruct((center_rows, outputs), f32),
            jax.ShapeDtypeStruct((eigen, outputs), f32),
            jax.ShapeDtypeStruct((eigen, 1), f32),
        ),
        in_specs=[hbm, hbm, vmem],
        out_specs=(vmem, vmem, vmem),
        scratch_shapes=[
            VMEM(kernel_here.shape, bf16),
            VMEM((1, eigen), f32),
            pltpu.SemaphoreType.DMA((2,)),
        ],
        compiler_params=small,
    )(
        pltpu.with_memory_space_constraint(kernel_here, pltpu.HBM),
        pltpu.with_memory_space_constraint(damping.reshape(1, eigen), pltpu.HBM),
        here,
    )
    steps = 4
    updated = pl.pallas_call(
        functools.partial(update, steps),
        out_shape=jax.ShapeDtypeStruct((center_rows, outputs), bf16),
        in_specs=[vmem] * 7,
        out_specs=hbm,
        scratch_shapes=[
            VMEM((center_rows, outputs), bf16),
            pltpu.SemaphoreType.DMA((steps,)),
        ],
        compiler_params=small,
    )(kernel_there, there, slope, projected, local_basis, damping, weights)
    return (updated, residual)


def solution(mesh):
    devices = mesh.devices
    fine = Mesh(
        devices.reshape(4, devices.shape[0] // 8, 2, devices.shape[1]),
        ("x", "z", "core", "batch"),
    )
    center = ("x", "z", "core")
    return jax.shard_map(
        per_device,
        mesh=fine,
        in_specs=(
            P(center, None),
            P(center, None),
            P(center),
            P(center, None),
            P(),
            P("batch", center, None),
            P("batch", center, None),
            P("batch", center),
        ),
        out_specs=(P(center, None), P("batch", center, None)),
        check_vma=False,
    )
```

```python
import functools

import jax
import jax.numpy as jnp
from jax import lax
from jax.experimental import pallas as pl
from jax.experimental.pallas import tpu as pltpu
from jax.sharding import Mesh, PartitionSpec as P

kernel_length = 2.0
step_rate = 0.1
f32 = jnp.float32
bf16 = jnp.bfloat16
i32 = jnp.int32
VMEM = pltpu.VMEM


def far_first(size):
    return [(k + size // 2) % size for k in range(size)]


def exchange(values, *axes):
    order = [0]
    for axis in axes:
        size = lax.axis_size(axis)
        own = range(size) if axis == "core" else far_first(size)
        order = [k * size + j for k in order for j in own]
    names = axes if len(axes) > 1 else axes[0]
    return lax.all_to_all(
        values, names, split_axis=0, concat_axis=0, tiled=True, axis_index_groups=[order]
    )


def spot(axis):
    size = lax.axis_size(axis)
    return lax.rem(lax.axis_index(axis) + size // 2, size)


def iota(shape, dim):
    return lax.broadcasted_iota(i32, shape, dim)


def mxu(left, right, contract=((1,), (0,))):
    return lax.dot_general(left, right, (contract, ((), ())), preferred_element_type=f32)


def rows_dot(left, right):
    return mxu(left, right, ((0,), (0,)))


def laplace(distance):
    return jnp.exp(-jnp.sqrt(jnp.maximum(distance, 0.0)) / kernel_length).astype(bf16)


def prepare(sizes, *refs):
    nx, nz, nc, rows_each, capacity = sizes
    out_ref, target_ref = refs[5:7]
    picks_ref, index_ref, basis_ref, stored_ref, label_ref, done = refs[7:]
    copies = [
        pltpu.make_async_copy(source, target, done.at[k])
        for k, (source, target) in enumerate(zip(refs[:5], refs[7:12]))
    ]
    for copy in copies:
        copy.start()
    for copy in copies:
        copy.wait()
    entries, eigen = basis_ref.shape
    group = spot("batch")
    upper = jnp.where(spot("x") < nx // 2, 0, eigen // 8)
    half = eigen // 2
    depth, width = stored_ref.shape
    index = index_ref[...]
    eye = iota((entries, entries), 0) == iota((entries, entries), 1)
    bits = rows_each.bit_length() - 1
    holder = lax.shift_right_logical(index, bits)
    column = jnp.sum(jnp.where(eye, index, 0), axis=1, keepdims=True)
    column_holder = lax.shift_right_logical(column, bits)
    column_row = lax.bitwise_and(column, rows_each - 1)
    earlier = iota((entries, entries), 0) > iota((entries, entries), 1)
    rank = jnp.sum(
        jnp.where((column_holder == holder) & earlier, 1, 0), axis=1, keepdims=True
    )
    lane = lax.bitwise_and(iota((entries, eigen), 1), half - 1)
    low = lax.bitwise_and(column_row, 255)
    high = lax.shift_right_logical(column_row, 8)
    digit = jnp.where(lax.bitwise_and(lane, 1) == 0, low, high)
    position = jnp.where(lax.shift_right_logical(lane, 1) == rank + upper, digit, 0).astype(f32)
    kept = jnp.where(rank == group, basis_ref[...].astype(f32), 0.0)
    carried = jnp.where(group < capacity, kept, position)
    carried = jnp.concatenate([carried[:, :half], carried[:, half:]], axis=0)
    line_bits = (nz * nc).bit_length() - 1
    across = lax.shift_right_logical(column_holder, line_bits)
    across = lax.bitwise_and(across + nx // 2, nx - 1)
    corner = across * nc + lax.bitwise_and(column_holder, nc - 1)
    corner = jnp.concatenate([corner, corner], axis=0)
    line = lax.shift_right_logical(lax.bitwise_and(holder, nz * nc - 1), nc.bit_length() - 1)
    line = lax.bitwise_and(line + nz // 2, nz - 1)
    here = iota((2 * nz, entries), 0)
    same = lax.shift_right_logical(here, 1) == line
    odd = lax.bitwise_and(here, 1)
    goal = jnp.concatenate(
        [jnp.where(same & (odd == h), 1.0, 0.0).astype(bf16) for h in range(2)], axis=1
    )
    sample = iota((2 * nz, depth), 0)
    wanted = jnp.where(lax.bitwise_and(sample, 1) == 0, picks_ref[0, 0], picks_ref[0, 1])
    picked = jnp.where(wanted == iota((2 * nz, depth), 1), 1.0, 0.0).astype(bf16)
    out_ref[:, :width] = mxu(picked, stored_ref[...]).astype(bf16)
    target_ref[...] = mxu(picked[: target_ref.shape[0], :], label_ref[...])
    for k in range(nx * nc):
        spread = jnp.where(corner == k, carried, 0.0).astype(bf16)
        out_ref[:, width + k * half : width + (k + 1) * half] = mxu(goal, spread).astype(bf16)


def squares(values):
    wide = values.astype(f32)
    return jnp.sum(wide * wide, axis=1, keepdims=True)


def as_row(column):
    return jnp.broadcast_to(column, (column.shape[0], 128)).T[:1, :]


def predict(sizes, place_ref, features_ref, kept_ref, pair_ref, centers_ref, weights_ref, *outs):
    nc, ny, capacity = sizes
    out_ref, basis_ref = outs
    core, group = place_ref[0], place_ref[1]
    other = nc - 1 - core
    count, width = features_ref.shape
    rows = centers_ref.shape[0]
    outputs = weights_ref.shape[1]
    side = count // ny
    parts = width // 128
    centers = centers_ref[...]
    line = as_row(squares(centers))

    def across(features):
        cross = mxu(features, centers, ((1,), (1,)))
        return laplace(squares(features) + line - 2.0 * cross)

    start = pl.multiple_of(group * side, side)
    far = jnp.concatenate(
        [
            pair_ref[other, pl.ds(pl.multiple_of(k * count + start, side), side), :]
            for k in range(parts)
        ],
        axis=1,
    )
    kernel = across(jnp.concatenate([features_ref[pl.ds(start, side), :], far], axis=0))

    at = iota((rows, side), 0)
    parity = lax.bitwise_and(iota((1, side), 1), 1)
    halves = [jnp.zeros((rows, 128), f32) for _ in range(2)]
    for c in range(2):
        if c == 0:
            blocks = [kept_ref[k * side : (k + 1) * side, :] for k in range(capacity)]
            digits = kept_ref[capacity * side :, :]
        else:
            first = parts * count
            blocks = [
                pair_ref[other, first + k * side : first + (k + 1) * side, :]
                for k in range(capacity)
            ]
            digits = pair_ref[other, first + capacity * side :, :]
        digits = digits.astype(f32)
        digits = jnp.concatenate([digits, digits], axis=0).T
        for k in range(capacity):
            low, high = (
                digits[2 * k + d : 2 * k + d + 1, :] + 256.0 * digits[2 * k + d + 1 : 2 * k + d + 2, :]
                for d in (0, 64)
            )
            place = jnp.where(iota((1, side), 1) < side // 2, low, high).astype(i32)
            for h in range(2):
                held = jnp.where(parity == h, place, -1)
                member = jnp.where(at == held, 1.0, 0.0).astype(bf16)
                halves[h] = halves[h] + mxu(member, blocks[k])
    local = jnp.concatenate(halves, axis=1).astype(bf16)
    basis_ref[...] = local
    for values, first in ((weights_ref[...], 0), (local, outputs)):
        product = mxu(kernel, values).astype(bf16)
        for k, to in ((0, core), (1, other)):
            spot_rows = pl.ds(pl.multiple_of(to * side, side), side)
            out_ref[spot_rows, first : first + values.shape[1]] = product[
                k * side : (k + 1) * side, :
            ]


def spread(place_ref, features_ref, pair_ref, centers_ref, here_ref, there_ref):
    other = 1 - place_ref[0]
    count, width = features_ref.shape
    centers = centers_ref[...]
    column = squares(centers)
    theirs = jnp.concatenate(
        [pair_ref[other, k * count : (k + 1) * count, :] for k in range(width // 128)], axis=1
    )
    for out_ref, features in ((here_ref, features_ref[...]), (there_ref, theirs)):
        cross = mxu(centers, features, ((1,), (1,)))
        out_ref[...] = laplace(column + as_row(squares(features)) - 2.0 * cross)


def begin(kernel_hbm, damping_hbm, here_ref, *refs):
    slope_ref, project_ref, column_ref, kernel_ref, damping_ref, done = refs
    outputs = slope_ref.shape[1]
    copies = [
        pltpu.make_async_copy(kernel_hbm, kernel_ref, done.at[0]),
        pltpu.make_async_copy(damping_hbm, damping_ref, done.at[1]),
    ]
    for copy in copies:
        copy.start()
    project_ref[...] = rows_dot(here_ref[:, outputs:], here_ref[:, :outputs])
    for copy in copies:
        copy.wait()
    slope_ref[...] = mxu(kernel_ref[...], here_ref[:, :outputs])
    row = damping_ref[...]
    column_ref[...] = jnp.broadcast_to(row, (128, row.shape[1])).T[:, :1]


def update(steps, kernel_ref, there_ref, slope_ref, project_ref, basis_ref, damping_ref, weights_ref, out_hbm, held, done):
    rows, outputs = weights_ref.shape
    total = project_ref[...] + rows_dot(there_ref[:, outputs:], there_ref[:, :outputs])
    scaled = (damping_ref[...] * total).astype(bf16)
    tall = rows // steps
    copies = []
    for k in range(steps):
        at = slice(k * tall, (k + 1) * tall)
        change = slope_ref[at, :] + mxu(kernel_ref[at, :], there_ref[:, :outputs])
        change = change - mxu(basis_ref[at, :], scaled)
        held[at, :] = (weights_ref[at, :].astype(f32) - step_rate * change).astype(bf16)
        copy = pltpu.make_async_copy(held.at[at, :], out_hbm.at[at, :], done.at[k])
        copy.start()
        copies.append(copy)
    for copy in copies:
        copy.wait()


def per_device(
    centers, weights, subset_index, basis, damping, stored_train_features, pool_labels, picks
):
    nx, nz, nc, ny = (lax.axis_size(a) for a in ("x", "z", "core", "batch"))
    devices = nx * nz * nc
    own_rows = picks.shape[1]
    center_rows, width = centers.shape
    outputs = weights.shape[1]
    entries, eigen = basis.shape
    capacity = 4 * entries // devices
    block = nz * own_rows
    side = nx * block
    wide = outputs + eigen
    half = eigen // 2
    group = spot("batch")
    core = lax.axis_index("core")
    smem = pl.BlockSpec(memory_space=pltpu.SMEM)
    vmem = pl.BlockSpec(memory_space=VMEM)
    hbm = pl.BlockSpec(memory_space=pltpu.HBM)
    small = pltpu.CompilerParams(vmem_limit_bytes=16 * 1024 * 1024)

    first, own_targets = pl.pallas_call(
        functools.partial(prepare, (nx, nz, nc, center_rows, capacity)),
        out_shape=(
            jax.ShapeDtypeStruct((block, width + nx * eigen), bf16),
            jax.ShapeDtypeStruct((min(8, block), outputs), f32),
        ),
        in_specs=[hbm] * 5,
        out_specs=(vmem, vmem),
        scratch_shapes=[
            pltpu.SMEM((1, own_rows), i32),
            VMEM((1, entries), i32),
            VMEM((entries, eigen), bf16),
            VMEM(stored_train_features.shape[1:], bf16),
            VMEM(pool_labels.shape[1:], bf16),
            pltpu.SemaphoreType.DMA((5,)),
        ],
        compiler_params=small,
    )(
        *(
            pltpu.with_memory_space_constraint(v, pltpu.HBM)
            for v in (
                picks,
                subset_index.reshape(1, entries),
                basis,
                stored_train_features[0],
                pool_labels[0],
            )
        )
    )
    first = first.reshape(nz, own_rows, width + nx * eigen)
    first, group, core = lax.optimization_barrier((first, group, core))
    first = exchange(first, "z").reshape(block, width + nx * eigen)
    second = jnp.stack(
        [
            jnp.concatenate(
                [first[:, :width], first[:, width + k * eigen : width + (k + 1) * eigen]], axis=1
            )
            for k in range(nx)
        ]
    )
    second = jnp.broadcast_to(second[None], (ny, nx, block, width + eigen))
    second, group, core = lax.optimization_barrier((second, group, core))
    second = exchange(second.reshape(ny * nx, block, width + eigen), "batch", "x")
    second, group, core = lax.optimization_barrier((second, group, core))
    features = second[:, :, :width].reshape(ny * side, width)
    near = second[:, :, width : width + half].reshape(ny * side, half)
    far = second[:, :, width + half :].reshape(ny * side, half)
    kept, sent = jnp.where(core == 0, near, far), jnp.where(core == 0, far, near)
    places = capacity * side
    kept, sent = (
        jnp.concatenate([v[:places], v[places : places + side // 2] + v[places + side // 2 :]])
        for v in (kept, sent)
    )
    pair = lax.all_gather(
        jnp.concatenate(
            [features[:, k : k + 128] for k in range(0, width, 128)] + [sent], axis=0
        ),
        "core",
    )
    place = jnp.stack([core, group])
    partial, local_basis = pl.pallas_call(
        functools.partial(predict, (nc, ny, capacity)),
        out_shape=(
            jax.ShapeDtypeStruct((nc * side, wide), bf16),
            jax.ShapeDtypeStruct((center_rows, eigen), bf16),
        ),
        in_specs=[smem, vmem, vmem, vmem, vmem, vmem],
        out_specs=(vmem, vmem),
        compiler_params=small,
    )(place, features, kept, pair, centers, weights)
    partial = exchange(partial.reshape(nc * nx, block, wide), "core", "x")
    partial = jnp.sum(partial.astype(f32), axis=0).astype(bf16)
    partial, place = lax.optimization_barrier((partial, place))
    partial = exchange(partial.reshape(nz, own_rows, wide), "z")
    square = jax.ShapeDtypeStruct((center_rows, ny * side), bf16)
    kernel_here, kernel_there = pl.pallas_call(
        spread,
        out_shape=(square, square),
        in_specs=[smem, vmem, vmem, vmem],
        out_specs=(vmem, vmem),
        compiler_params=small,
    )(place, features, pair, centers)
    total = jnp.sum(partial.astype(f32), axis=0)
    residual = (total[:, :outputs] - own_targets[:own_rows]).astype(bf16)
    own = jnp.concatenate([residual, total[:, outputs:].astype(bf16)], axis=1)
    own, kernel_here, kernel_there = lax.optimization_barrier((own, kernel_here, kernel_there))

    own_all = exchange(jnp.broadcast_to(own[None], (nz, own_rows, wide)), "z")
    own_all = jnp.broadcast_to(own_all.reshape(1, block, wide), (ny * nx, block, wide))
    here = exchange(own_all, "batch", "x")
    residual = lax.dynamic_slice(
        here,
        (spot("batch") * nx + spot("x"), spot("z") * own_rows, 0),
        (1, own_rows, outputs),
    )
    here = here.reshape(ny * side, wide)
    there = lax.ppermute(here, "core", [(k, nc - 1 - k) for k in range(nc)])
    slope, projected, damping = pl.pallas_call(
        begin,
        out_shape=(
            jax.ShapeDtypeStruct((center_rows, outputs), f32),
            jax.ShapeDtypeStruct((eigen, outputs), f32),
            jax.ShapeDtypeStruct((eigen, 1), f32),
        ),
        in_specs=[hbm, hbm, vmem],
        out_specs=(vmem, vmem, vmem),
        scratch_shapes=[
            VMEM(kernel_here.shape, bf16),
            VMEM((1, eigen), f32),
            pltpu.SemaphoreType.DMA((2,)),
        ],
        compiler_params=small,
    )(
        pltpu.with_memory_space_constraint(kernel_here, pltpu.HBM),
        pltpu.with_memory_space_constraint(damping.reshape(1, eigen), pltpu.HBM),
        here,
    )
    steps = 2
    updated = pl.pallas_call(
        functools.partial(update, steps),
        out_shape=jax.ShapeDtypeStruct((center_rows, outputs), bf16),
        in_specs=[vmem] * 7,
        out_specs=hbm,
        scratch_shapes=[
            VMEM((center_rows, outputs), bf16),
            pltpu.SemaphoreType.DMA((steps,)),
        ],
        compiler_params=small,
    )(kernel_there, there, slope, projected, local_basis, damping, weights)
    return (updated, residual)


def solution(mesh):
    devices = mesh.devices
    fine = Mesh(
        devices.reshape(4, devices.shape[0] // 8, 2, devices.shape[1]),
        ("x", "z", "core", "batch"),
    )
    center = ("x", "z", "core")
    return jax.shard_map(
        per_device,
        mesh=fine,
        in_specs=(
            P(center, None),
            P(center, None),
            P(center),
            P(center, None),
            P(),
            P("batch", center, None),
            P("batch", center, None),
            P("batch", center),
        ),
        out_specs=(P(center, None), P("batch", center, None)),
        check_vma=False,
    )
```

```python
import functools

import jax
import jax.numpy as jnp
from jax import lax
from jax.experimental import pallas as pl
from jax.experimental.pallas import tpu as pltpu
from jax.sharding import Mesh, PartitionSpec as P

kernel_length = 2.0
step_rate = 0.1
f32 = jnp.float32
bf16 = jnp.bfloat16
i32 = jnp.int32
VMEM = pltpu.VMEM


def origin(axis, size):
    return 5 * size // 8 if axis == "z" else size // 2


def far_first(axis, size):
    return [(k + origin(axis, size)) % size for k in range(size)]


def exchange(values, *axes):
    order = [0]
    for axis in axes:
        size = lax.axis_size(axis)
        own = range(size) if axis == "core" else far_first(axis, size)
        order = [k * size + j for k in order for j in own]
    names = axes if len(axes) > 1 else axes[0]
    return lax.all_to_all(
        values, names, split_axis=0, concat_axis=0, tiled=True, axis_index_groups=[order]
    )


def spot(axis):
    size = lax.axis_size(axis)
    return lax.rem(lax.axis_index(axis) + size - origin(axis, size), size)


def iota(shape, dim):
    return lax.broadcasted_iota(i32, shape, dim)


def mxu(left, right, contract=((1,), (0,))):
    return lax.dot_general(left, right, (contract, ((), ())), preferred_element_type=f32)


def rows_dot(left, right):
    return mxu(left, right, ((0,), (0,)))


def laplace(distance):
    return jnp.exp(-jnp.sqrt(jnp.maximum(distance, 0.0)) / kernel_length).astype(bf16)


def prepare(sizes, *refs):
    nx, nz, nc, rows_each, capacity = sizes
    out_ref, target_ref = refs[5:7]
    picks_ref, index_ref, basis_ref, stored_ref, label_ref, done = refs[7:]
    copies = [
        pltpu.make_async_copy(source, target, done.at[k])
        for k, (source, target) in enumerate(zip(refs[:5], refs[7:12]))
    ]
    for copy in copies:
        copy.start()
    for copy in copies:
        copy.wait()
    entries, eigen = basis_ref.shape
    group = spot("batch")
    upper = jnp.where(spot("x") < nx // 2, 0, eigen // 8)
    half = eigen // 2
    depth, width = stored_ref.shape
    index = index_ref[...]
    eye = iota((entries, entries), 0) == iota((entries, entries), 1)
    bits = rows_each.bit_length() - 1
    holder = lax.shift_right_logical(index, bits)
    column = jnp.sum(jnp.where(eye, index, 0), axis=1, keepdims=True)
    column_holder = lax.shift_right_logical(column, bits)
    column_row = lax.bitwise_and(column, rows_each - 1)
    earlier = iota((entries, entries), 0) > iota((entries, entries), 1)
    rank = jnp.sum(
        jnp.where((column_holder == holder) & earlier, 1, 0), axis=1, keepdims=True
    )
    lane = lax.bitwise_and(iota((entries, eigen), 1), half - 1)
    low = lax.bitwise_and(column_row, 255)
    high = lax.shift_right_logical(column_row, 8)
    digit = jnp.where(lax.bitwise_and(lane, 1) == 0, low, high)
    position = jnp.where(lax.shift_right_logical(lane, 1) == rank + upper, digit, 0).astype(f32)
    kept = jnp.where(rank == group, basis_ref[...].astype(f32), 0.0)
    carried = jnp.where(group < capacity, kept, position)
    carried = jnp.concatenate([carried[:, :half], carried[:, half:]], axis=0)
    line_bits = (nz * nc).bit_length() - 1
    across = lax.shift_right_logical(column_holder, line_bits)
    across = lax.bitwise_and(across + nx // 2, nx - 1)
    corner = across * nc + lax.bitwise_and(column_holder, nc - 1)
    corner = jnp.concatenate([corner, corner], axis=0)
    line = lax.shift_right_logical(lax.bitwise_and(holder, nz * nc - 1), nc.bit_length() - 1)
    line = lax.bitwise_and(line + nz - origin("z", nz), nz - 1)
    here = iota((2 * nz, entries), 0)
    same = lax.shift_right_logical(here, 1) == line
    odd = lax.bitwise_and(here, 1)
    goal = jnp.concatenate(
        [jnp.where(same & (odd == h), 1.0, 0.0).astype(bf16) for h in range(2)], axis=1
    )
    sample = iota((2 * nz, depth), 0)
    wanted = jnp.where(lax.bitwise_and(sample, 1) == 0, picks_ref[0, 0], picks_ref[0, 1])
    picked = jnp.where(wanted == iota((2 * nz, depth), 1), 1.0, 0.0).astype(bf16)
    out_ref[:, :width] = mxu(picked, stored_ref[...]).astype(bf16)
    target_ref[...] = mxu(picked[: target_ref.shape[0], :], label_ref[...])
    for k in range(nx * nc):
        spread = jnp.where(corner == k, carried, 0.0).astype(bf16)
        out_ref[:, width + k * half : width + (k + 1) * half] = mxu(goal, spread).astype(bf16)


def squares(values):
    wide = values.astype(f32)
    return jnp.sum(wide * wide, axis=1, keepdims=True)


def as_row(column):
    return jnp.broadcast_to(column, (column.shape[0], 128)).T[:1, :]


def predict(sizes, place_ref, features_ref, kept_ref, pair_ref, centers_ref, weights_ref, *outs):
    nc, ny, capacity = sizes
    out_ref, basis_ref = outs
    core, group = place_ref[0], place_ref[1]
    other = nc - 1 - core
    count, width = features_ref.shape
    rows = centers_ref.shape[0]
    outputs = weights_ref.shape[1]
    side = count // ny
    parts = width // 128
    centers = centers_ref[...]
    line = as_row(squares(centers))

    def across(features):
        cross = mxu(features, centers, ((1,), (1,)))
        return laplace(squares(features) + line - 2.0 * cross)

    start = pl.multiple_of(group * side, side)
    far = jnp.concatenate(
        [
            pair_ref[other, pl.ds(pl.multiple_of(k * count + start, side), side), :]
            for k in range(parts)
        ],
        axis=1,
    )
    kernel = across(jnp.concatenate([features_ref[pl.ds(start, side), :], far], axis=0))

    at = iota((rows, side), 0)
    parity = lax.bitwise_and(iota((1, side), 1), 1)
    halves = [jnp.zeros((rows, 128), f32) for _ in range(2)]
    for c in range(2):
        if c == 0:
            blocks = [kept_ref[k * side : (k + 1) * side, :] for k in range(capacity)]
            digits = kept_ref[capacity * side :, :]
        else:
            first = parts * count
            blocks = [
                pair_ref[other, first + k * side : first + (k + 1) * side, :]
                for k in range(capacity)
            ]
            digits = pair_ref[other, first + capacity * side :, :]
        digits = digits.astype(f32)
        digits = jnp.concatenate([digits, digits], axis=0).T
        for k in range(capacity):
            low, high = (
                digits[2 * k + d : 2 * k + d + 1, :] + 256.0 * digits[2 * k + d + 1 : 2 * k + d + 2, :]
                for d in (0, 64)
            )
            place = jnp.where(iota((1, side), 1) < side // 2, low, high).astype(i32)
            for h in range(2):
                held = jnp.where(parity == h, place, -1)
                member = jnp.where(at == held, 1.0, 0.0).astype(bf16)
                halves[h] = halves[h] + mxu(member, blocks[k])
    local = jnp.concatenate(halves, axis=1).astype(bf16)
    basis_ref[...] = local
    for values, first in ((weights_ref[...], 0), (local, outputs)):
        product = mxu(kernel, values).astype(bf16)
        for k, to in ((0, core), (1, other)):
            spot_rows = pl.ds(pl.multiple_of(to * side, side), side)
            out_ref[spot_rows, first : first + values.shape[1]] = product[
                k * side : (k + 1) * side, :
            ]


def spread(place_ref, features_ref, pair_ref, centers_ref, here_ref, there_ref):
    other = 1 - place_ref[0]
    count, width = features_ref.shape
    centers = centers_ref[...]
    column = squares(centers)
    theirs = jnp.concatenate(
        [pair_ref[other, k * count : (k + 1) * count, :] for k in range(width // 128)], axis=1
    )
    for out_ref, features in ((here_ref, features_ref[...]), (there_ref, theirs)):
        cross = mxu(centers, features, ((1,), (1,)))
        out_ref[...] = laplace(column + as_row(squares(features)) - 2.0 * cross)


def begin(kernel_hbm, damping_hbm, here_ref, *refs):
    slope_ref, project_ref, column_ref, kernel_ref, damping_ref, done = refs
    outputs = slope_ref.shape[1]
    copies = [
        pltpu.make_async_copy(kernel_hbm, kernel_ref, done.at[0]),
        pltpu.make_async_copy(damping_hbm, damping_ref, done.at[1]),
    ]
    for copy in copies:
        copy.start()
    project_ref[...] = rows_dot(here_ref[:, outputs:], here_ref[:, :outputs])
    for copy in copies:
        copy.wait()
    slope_ref[...] = mxu(kernel_ref[...], here_ref[:, :outputs])
    row = damping_ref[...]
    column_ref[...] = jnp.broadcast_to(row, (128, row.shape[1])).T[:, :1]


def update(steps, kernel_ref, there_ref, slope_ref, project_ref, basis_ref, damping_ref, weights_ref, out_hbm, held, done):
    rows, outputs = weights_ref.shape
    total = project_ref[...] + rows_dot(there_ref[:, outputs:], there_ref[:, :outputs])
    scaled = (damping_ref[...] * total).astype(bf16)
    tall = rows // steps
    copies = []
    for k in range(steps):
        at = slice(k * tall, (k + 1) * tall)
        change = slope_ref[at, :] + mxu(kernel_ref[at, :], there_ref[:, :outputs])
        change = change - mxu(basis_ref[at, :], scaled)
        held[at, :] = (weights_ref[at, :].astype(f32) - step_rate * change).astype(bf16)
        copy = pltpu.make_async_copy(held.at[at, :], out_hbm.at[at, :], done.at[k])
        copy.start()
        copies.append(copy)
    for copy in copies:
        copy.wait()


def per_device(
    centers, weights, subset_index, basis, damping, stored_train_features, pool_labels, picks
):
    nx, nz, nc, ny = (lax.axis_size(a) for a in ("x", "z", "core", "batch"))
    devices = nx * nz * nc
    own_rows = picks.shape[1]
    center_rows, width = centers.shape
    outputs = weights.shape[1]
    entries, eigen = basis.shape
    capacity = 4 * entries // devices
    block = nz * own_rows
    side = nx * block
    wide = outputs + eigen
    half = eigen // 2
    group = spot("batch")
    core = lax.axis_index("core")
    smem = pl.BlockSpec(memory_space=pltpu.SMEM)
    vmem = pl.BlockSpec(memory_space=VMEM)
    hbm = pl.BlockSpec(memory_space=pltpu.HBM)
    small = pltpu.CompilerParams(vmem_limit_bytes=16 * 1024 * 1024)

    first, own_targets = pl.pallas_call(
        functools.partial(prepare, (nx, nz, nc, center_rows, capacity)),
        out_shape=(
            jax.ShapeDtypeStruct((block, width + nx * eigen), bf16),
            jax.ShapeDtypeStruct((min(8, block), outputs), f32),
        ),
        in_specs=[hbm] * 5,
        out_specs=(vmem, vmem),
        scratch_shapes=[
            pltpu.SMEM((1, own_rows), i32),
            VMEM((1, entries), i32),
            VMEM((entries, eigen), bf16),
            VMEM(stored_train_features.shape[1:], bf16),
            VMEM(pool_labels.shape[1:], bf16),
            pltpu.SemaphoreType.DMA((5,)),
        ],
        compiler_params=small,
    )(
        *(
            pltpu.with_memory_space_constraint(v, pltpu.HBM)
            for v in (
                picks,
                subset_index.reshape(1, entries),
                basis,
                stored_train_features[0],
                pool_labels[0],
            )
        )
    )
    first = first.reshape(nz, own_rows, width + nx * eigen)
    first, group, core = lax.optimization_barrier((first, group, core))
    first = exchange(first, "z").reshape(block, width + nx * eigen)
    second = jnp.stack(
        [
            jnp.concatenate(
                [first[:, :width], first[:, width + k * eigen : width + (k + 1) * eigen]], axis=1
            )
            for k in range(nx)
        ]
    )
    second = jnp.broadcast_to(second[None], (ny, nx, block, width + eigen))
    second, group, core = lax.optimization_barrier((second, group, core))
    second = exchange(second.reshape(ny * nx, block, width + eigen), "batch", "x")
    second, group, core = lax.optimization_barrier((second, group, core))
    features = second[:, :, :width].reshape(ny * side, width)
    near = second[:, :, width : width + half].reshape(ny * side, half)
    far = second[:, :, width + half :].reshape(ny * side, half)
    kept, sent = jnp.where(core == 0, near, far), jnp.where(core == 0, far, near)
    places = capacity * side
    kept, sent = (
        jnp.concatenate([v[:places], v[places : places + side // 2] + v[places + side // 2 :]])
        for v in (kept, sent)
    )
    pair = lax.all_gather(
        jnp.concatenate(
            [features[:, k : k + 128] for k in range(0, width, 128)] + [sent], axis=0
        ),
        "core",
    )
    place = jnp.stack([core, group])
    partial, local_basis = pl.pallas_call(
        functools.partial(predict, (nc, ny, capacity)),
        out_shape=(
            jax.ShapeDtypeStruct((nc * side, wide), bf16),
            jax.ShapeDtypeStruct((center_rows, eigen), bf16),
        ),
        in_specs=[smem, vmem, vmem, vmem, vmem, vmem],
        out_specs=(vmem, vmem),
        compiler_params=small,
    )(place, features, kept, pair, centers, weights)
    partial = exchange(partial.reshape(nc * nx, block, wide), "core", "x")
    partial = jnp.sum(partial.astype(f32), axis=0).astype(bf16)
    partial, place = lax.optimization_barrier((partial, place))
    partial = exchange(partial.reshape(nz, own_rows, wide), "z")
    square = jax.ShapeDtypeStruct((center_rows, ny * side), bf16)
    kernel_here, kernel_there = pl.pallas_call(
        spread,
        out_shape=(square, square),
        in_specs=[smem, vmem, vmem, vmem],
        out_specs=(vmem, vmem),
        compiler_params=small,
    )(place, features, pair, centers)
    total = jnp.sum(partial.astype(f32), axis=0)
    residual = (total[:, :outputs] - own_targets[:own_rows]).astype(bf16)
    own = jnp.concatenate([residual, total[:, outputs:].astype(bf16)], axis=1)
    own, kernel_here, kernel_there = lax.optimization_barrier((own, kernel_here, kernel_there))

    own_all = exchange(jnp.broadcast_to(own[None], (nz, own_rows, wide)), "z")
    own_all = jnp.broadcast_to(own_all.reshape(1, block, wide), (ny * nx, block, wide))
    here = exchange(own_all, "batch", "x")
    residual = lax.dynamic_slice(
        here,
        (spot("batch") * nx + spot("x"), spot("z") * own_rows, 0),
        (1, own_rows, outputs),
    )
    here = here.reshape(ny * side, wide)
    there = lax.ppermute(here, "core", [(k, nc - 1 - k) for k in range(nc)])
    slope, projected, damping = pl.pallas_call(
        begin,
        out_shape=(
            jax.ShapeDtypeStruct((center_rows, outputs), f32),
            jax.ShapeDtypeStruct((eigen, outputs), f32),
            jax.ShapeDtypeStruct((eigen, 1), f32),
        ),
        in_specs=[hbm, hbm, vmem],
        out_specs=(vmem, vmem, vmem),
        scratch_shapes=[
            VMEM(kernel_here.shape, bf16),
            VMEM((1, eigen), f32),
            pltpu.SemaphoreType.DMA((2,)),
        ],
        compiler_params=small,
    )(
        pltpu.with_memory_space_constraint(kernel_here, pltpu.HBM),
        pltpu.with_memory_space_constraint(damping.reshape(1, eigen), pltpu.HBM),
        here,
    )
    steps = 2
    updated = pl.pallas_call(
        functools.partial(update, steps),
        out_shape=jax.ShapeDtypeStruct((center_rows, outputs), bf16),
        in_specs=[vmem] * 7,
        out_specs=hbm,
        scratch_shapes=[
            VMEM((center_rows, outputs), bf16),
            pltpu.SemaphoreType.DMA((steps,)),
        ],
        compiler_params=small,
    )(kernel_there, there, slope, projected, local_basis, damping, weights)
    return (updated, residual)


def solution(mesh):
    devices = mesh.devices
    fine = Mesh(
        devices.reshape(4, devices.shape[0] // 8, 2, devices.shape[1]),
        ("x", "z", "core", "batch"),
    )
    center = ("x", "z", "core")
    return jax.shard_map(
        per_device,
        mesh=fine,
        in_specs=(
            P(center, None),
            P(center, None),
            P(center),
            P(center, None),
            P(),
            P("batch", center, None),
            P("batch", center, None),
            P("batch", center),
        ),
        out_specs=(P(center, None), P("batch", center, None)),
        check_vma=False,
    )
```
